256 devices in a mesh: row: 32 (over z, y), col: 8 (over x, core).
Axes of the slice: x: 4, y: 4, z: 8, core: 2. Of those that a mesh axis runs over, the one named last changes fastest.
Arguments:
- anc_factor: float32 [32768, 8192], P('row', 'col'), may hold values from -0.046875 to 0.046875
- anc_solution: float32 [128, 49152], P('col', 'row'), may hold values from -6 to 6
- slot_row: int32 [32768], P('row'), may hold values from 0 to 1535, as said below
- tile_count: int32 [32], P('row'), may hold values from 2 to 8, as said below
- lower_factor: float32 [8, 1024, 8192], P(None, 'row', 'col'), may hold values from -0.109375 to 0.109375
- diag_inverse: float32 [8, 1024, 1024], P('col'), may hold values from -1.5 to 1.5, as said below
- rhs: float32 [128, 8192], P('row', 'col'), may hold values from -6 to 6
Outputs:
- solution: float32 [128, 8192], P('row', 'col')
The draws below stay inside these ranges and needn't reach their ends.
Inputs may be any that keep to these rules, and one draw needn't show every extreme that they name: `slot_row`: within each aligned block of 1024 entries the values are distinct, and some block holds 1535. `tile_count`: some entry equals 8 in every draw. Each block diag_inverse[t] is lower triangular with a positive diagonal.
All inputs are finite; a program needn't handle non-finite values.
Results may differ from the reference program's by a relative error of at most 0.0001.
Values sent between devices are 32-bit elements; how exact they have to be, the bound alone decides.
No kernel may reach another device: no remote copies, remote signals or barrier semaphores. Data moves between devices by JAX's collectives and lax.ppermute only.
A program may use at most 64 MiB of HBM per device.

```python
import math
import jax
import jax.numpy as jnp
from jax import lax

PW = 1024
TILE = 128
TILES_DEV = 8
ANC_DEV = 1536
RHS = 128
SLOTS_DEV = 1024
PANELS = 8
NPIV = 8192
ANC_ROWS = 32768
PARENT_ROWS = 49152
N_ROW = 32


def draw_slot_row(key, part):
    count_rows = ANC_ROWS // SLOTS_DEV
    keys_all = jax.random.split(key, count_rows)

    def one_device(device_key):
        chosen = jax.random.permutation(device_key, ANC_DEV)[:SLOTS_DEV]
        present = jnp.any(chosen == ANC_DEV - 1)
        return jnp.where(present, chosen, chosen.at[SLOTS_DEV - 1].set(ANC_DEV - 1))
    return jax.vmap(one_device)(keys_all).reshape(-1).astype(jnp.int32)


def draw_tile_count(key, part):
    key_counts, key_pick = jax.random.split(jax.random.fold_in(key, 7))
    count_rows = ANC_ROWS // SLOTS_DEV
    counts = jax.random.randint(key_counts, (count_rows,), TILES_DEV // 4, TILES_DEV // 2 + 1)
    busiest = jax.random.randint(key_pick, (), 0, count_rows)
    return jnp.where(jnp.arange(count_rows) == busiest, TILES_DEV, counts).astype(jnp.int32)


def draw_diag_inverse(key, part):
    key_lower, key_diag = jax.random.split(jax.random.fold_in(key, 11))
    spread = jnp.clip(jax.random.normal(key_lower, (PANELS, PW, PW), jnp.float32), -2.5, 2.5)
    lower_part = jnp.tril(spread, -1) * (0.6 / math.sqrt(PW))
    diagonal = jax.random.uniform(key_diag, (PANELS, PW), jnp.float32, 0.6, 1.4)
    return lower_part + diagonal[:, :, None] * jnp.eye(PW, dtype=jnp.float32)[None, :, :]


def block_levels(own_key, extent, cuts, low, largest):
    factor_of, own = 1.0, jax.random.fold_in(own_key, 6)
    for dim, parts in cuts:
        heights = jnp.exp(jax.random.uniform(jax.random.fold_in(own, dim), (parts,), jnp.float32, low / len(cuts), largest / len(cuts)))
        factor_of = factor_of * jnp.repeat(heights, extent[dim] // parts).reshape([-1 if axis == dim else 1 for axis in range(len(extent))])
    return factor_of


def scatter_about(rng, extent, scale, limit, shards=(), kind=jnp.bfloat16):
    array = jax.random.normal(rng, extent, jnp.float32) * scale
    if len(shards) > 0:
        array = block_levels(rng, extent, shards, -0.22, 0.18) * array
    return jnp.clip(array, min=-limit, max=limit).astype(kind)


def setup_inputs(seed: int = 0) -> dict:
    key_list = jax.random.split(jax.random.key(seed), 8)
    anc_factor = scatter_about(key_list[0], (ANC_ROWS, NPIV), (ANC_ROWS // 2) ** -0.5, 0.046875, ((0, 32), (1, 8)), jnp.float32)
    anc_solution = scatter_about(key_list[1], (RHS, PARENT_ROWS), 1.0, 6.0, ((0, 8), (1, 32)), jnp.float32)
    slot_row = draw_slot_row(jax.random.fold_in(key_list[7], 71), 0)
    tile_count = draw_tile_count(jax.random.fold_in(key_list[7], 71), 0)
    lower_factor = scatter_about(key_list[4], (PANELS, PW, NPIV), (3 * PW) ** -0.5, 0.109375, ((1, 32), (2, 8)), jnp.float32)
    diag_inverse = draw_diag_inverse(jax.random.fold_in(key_list[7], 71), 0)
    rhs = scatter_about(key_list[6], (RHS, NPIV), 1.0, 6.0, ((0, 32), (1, 8)), jnp.float32)
    return dict(anc_factor=anc_factor, anc_solution=anc_solution, slot_row=slot_row, tile_count=tile_count, lower_factor=lower_factor, diag_inverse=diag_inverse, rhs=rhs)


def reference(anc_factor, anc_solution, slot_row, tile_count, lower_factor, diag_inverse, rhs):
    highest = lax.Precision.HIGHEST
    position = jnp.arange(N_ROW * SLOTS_DEV).astype(jnp.int32)
    owner_row = position // SLOTS_DEV
    parent_index = (owner_row * ANC_DEV + slot_row).astype(jnp.int32)
    alive_mask = ((position % SLOTS_DEV) < tile_count[owner_row] * TILE).astype(jnp.float32)
    selected = jnp.take(anc_solution, parent_index, axis=1) * alive_mask[None, :]
    updated = rhs - jnp.dot(selected, anc_factor, precision=highest, preferred_element_type=jnp.float32)
    solution = jnp.zeros((RHS, NPIV), jnp.float32)
    for target in range(PANELS - 1, -1, -1):
        offset = target * PW
        pending = updated[:, offset:offset + PW]
        if target < PANELS - 1:
            below_rows = lower_factor[target + 1:, :, offset:offset + PW].reshape(-1, PW)
            pending = pending - jnp.dot(solution[:, offset + PW:], below_rows, precision=highest, preferred_element_type=jnp.float32)
        solved = jnp.dot(pending, diag_inverse[target], precision=highest, preferred_element_type=jnp.float32)
        solution = solution.at[:, offset:offset + PW].set(solved)
    return solution
```

```python
import jax
import jax.numpy as jnp
from jax import lax
from jax.sharding import PartitionSpec as P

TILE = 128
HALF = 4


def dot(a, b, precision=lax.Precision.HIGHEST):
    return jnp.dot(a, b, precision=precision, preferred_element_type=jnp.float32)


def scatter_rows(partial_sum):
    rows = lax.axis_size("row")
    parts = partial_sum.reshape(rows, -1, partial_sum.shape[1])
    return lax.all_to_all(parts, "row", 0, 0).sum(axis=0)


def on_device(anc_factor, anc_solution, slot_row, tile_count, lower_factor, diag_inverse, rhs):
    column = lax.axis_index("col")
    panels, rows_local, width = lower_factor.shape
    base = column // HALF * HALF
    place = column % HALF
    diag = diag_inverse[0]

    scaled = dot(lower_factor.reshape(panels * rows_local, width), diag)
    scaled = scaled.reshape(panels, rows_local, width)

    def block(k):
        return lax.dynamic_index_in_dim(scaled, k, 0, keepdims=False)

    own = block(base + jnp.where(place == 0, 3, 2))
    lent = lax.ppermute(
        block(base + jnp.where(place == 0, 2, 3)), "col", [(0, 2), (1, 3), (4, 6), (5, 7)]
    )
    between = jnp.where(place < 2, own, lent)
    within = block(jnp.minimum(column + 1, panels - 1))
    near = lax.all_gather(
        jnp.concatenate([between, within], axis=1), "row", axis=0, tiled=True
    )

    alive = jnp.arange(slot_row.shape[0]) < tile_count[0] * TILE
    mine = jnp.where(alive[None, :], jnp.take(anc_solution, slot_row, axis=1), 0.0)
    chosen = lax.all_gather(mine, "col", axis=0, tiled=True)
    updated = rhs - scatter_rows(dot(chosen, anc_factor))
    value = dot(updated, diag)

    between_full = near[:, :width]
    within_full = near[:, width:]

    def inside_pair(value, source):
        got = lax.ppermute(value, "col", [(source, source - 1)])
        return value - dot(got, within_full, lax.Precision.HIGH)

    def solve_half(value, low):
        a, b, c, d = low, low + 1, low + 2, low + 3
        value = inside_pair(value, d)
        got = lax.ppermute(value, "col", [(d, a), (c, b)])
        upper = (column == c) | (column == d)
        term = dot(jnp.where(upper, value, got), between_full, lax.Precision.HIGH)
        back = lax.ppermute(term, "col", [(d, b), (c, a)])
        lower = (column == a) | (column == b)
        value = value - jnp.where(lower, term + back, 0.0)
        return inside_pair(value, b)

    value = solve_half(value, HALF)

    spread = lax.all_to_all(value, "row", split_axis=1, concat_axis=0, tiled=True)
    known, weights = [], []
    for shift in range(HALF):
        pairs = [(HALF + (i + shift) % HALF, i) for i in range(HALF)]
        known.append(lax.ppermute(spread, "col", pairs))
        weights.append(block(HALF + (place + shift) % HALF))
    term = dot(jnp.concatenate(known, axis=1), jnp.concatenate(weights, axis=0))
    value = value - scatter_rows(term)

    return solve_half(value, 0)


def solution(mesh):
    in_specs = (
        P("row", "col"),
        P("col", "row"),
        P("row"),
        P("row"),
        P(None, "row", "col"),
        P("col", None, None),
        P("row", "col"),
    )
    out_specs = P("row", "col")
    return jax.shard_map(
        on_device, mesh=mesh, in_specs=in_specs, out_specs=out_specs, check_vma=False
    )
```

```python
import jax
import jax.numpy as jnp
from jax import lax
from jax.sharding import PartitionSpec as P


TILE = 128
HALF = 4
DEPTH = 4


def dot(a, b, precision=lax.Precision.HIGHEST):
    return jnp.dot(a, b, precision=precision, preferred_element_type=jnp.float32)


def z_groups(rows):
    return [list(range(y, rows, DEPTH)) for y in range(DEPTH)]


def y_shift(rows, by):
    return [(r // DEPTH * DEPTH + (r + by) % DEPTH, r) for r in range(rows)]


def send_y(array, rows):
    return [array] + [lax.ppermute(array, "row", y_shift(rows, by)) for by in range(1, DEPTH)]


def join_y(parts):
    y = lax.axis_index("row") % DEPTH
    whole = jnp.zeros((DEPTH,) + parts[0].shape, parts[0].dtype)
    for by, part in enumerate(parts):
        whole = lax.dynamic_update_index_in_dim(whole, part, (y + by) % DEPTH, 0)
    return whole


def scatter_z(parts, rows):
    return lax.all_to_all(parts, "row", 0, 0, axis_index_groups=z_groups(rows)).sum(axis=0)


def scatter_rows(partial_sum, rows):
    parts = partial_sum.reshape(rows, -1, partial_sum.shape[1])
    return lax.all_to_all(parts, "row", 0, 0).sum(axis=0)


def on_device(anc_factor, anc_solution, slot_row, tile_count, lower_factor, diag_inverse, rhs):
    column = lax.axis_index("col")
    rows = lax.axis_size("row")
    panels, rows_local, width = lower_factor.shape
    diag = diag_inverse[0]

    scaled = dot(lower_factor.reshape(panels * rows_local, width), diag)
    scaled = scaled.reshape(panels, rows_local, width)
    block = lambda k: lax.dynamic_index_in_dim(scaled, k, 0, keepdims=False)

    own = block(jnp.minimum(column + 1, panels - 1))
    one = block(jnp.where(column < HALF, 2, 7))
    two = block(jnp.where(column < HALF, 3, 6))
    one = lax.ppermute(one, "col", [(5, 7), (4, 3), (0, 6)])
    two = lax.ppermute(two, "col", [(4, 2), (1, 3), (0, 7)])
    upper = jnp.where(column == 2, two, one)
    upper = jnp.where((column >= 4) & (column <= 6), own, upper)
    lower = jnp.where(column == 6, one, two)
    lower = jnp.where(column <= 2, own, lower)

    def near_full(share):
        return lax.all_gather(
            share.reshape(-1, width),
            "row",
            axis=0,
            tiled=True,
            axis_index_groups=z_groups(rows),
        )

    upper = send_y(upper, rows)
    twice = jnp.concatenate([scaled[HALF:], scaled[HALF:-1]], axis=0)
    far = lax.dynamic_slice_in_dim(twice, column % HALF, HALF, 0)
    rest = send_y(jnp.concatenate([lower[None], far], axis=0), rows)
    upper_near = near_full(join_y(upper))

    alive = jnp.arange(slot_row.shape[0]) < tile_count[0] * TILE
    mine = jnp.where(alive[None, :], jnp.take(anc_solution, slot_row, axis=1), 0.0)
    chosen = lax.all_gather(mine, "col", axis=0, tiled=True)
    total = scatter_rows(dot(chosen, anc_factor), rows)
    value = dot(rhs - total, diag)
    value, rest = lax.optimization_barrier((value, rest))
    lower_near = near_full(join_y([lower] + [part[0] for part in rest[1:]]))

    def solve_half(value, low, near):
        a, b, c, d = low, low + 1, low + 2, low + 3
        first, second = (low + 7) % panels, (low + 6) % panels

        def send(array, pairs):
            return lax.ppermute(array, "col", pairs)

        def times(array):
            return dot(array, near, lax.Precision.HIGH)

        got = send(value, [(d, c)]) + send(value, [(d, first)])
        term = times(jnp.where(column == d, value, got))
        value = value - jnp.where(column == c, term, 0.0)
        aside = send(term, [(d, b), (first, a)])
        got = send(value, [(c, b)]) + send(value, [(c, second)])
        term = times(got)
        term, aside = lax.optimization_barrier((term, aside))
        value = value - jnp.where(column == b, term, 0.0) - aside
        aside = send(term, [(second, a)])
        term = times(send(value, [(b, a)]))
        term, aside = lax.optimization_barrier((term, aside))
        return value - term - aside

    value = solve_half(value, HALF, upper_near)
    value, rest = lax.optimization_barrier((value, rest))
    far_full = join_y([far] + [part[1:] for part in rest[1:]]).transpose(1, 0, 2, 3).reshape(-1, width)

    known = []
    for shift in range(HALF):
        pairs = [(HALF + (i + shift) % HALF, i) for i in range(HALF)]
        known.append(lax.ppermute(value, "col", pairs))
    depth = rows // DEPTH
    shares = value.shape[0]
    known = jnp.stack(known).reshape(HALF, shares, depth, -1).transpose(2, 1, 0, 3)
    known = lax.all_to_all(known, "row", 0, 0, axis_index_groups=z_groups(rows))
    term = dot(known.reshape(depth * shares, -1), far_full)
    value = value - scatter_z(term.reshape(depth, shares, width), rows)

    return solve_half(value, 0, lower_near)


def solution(mesh):
    in_specs = (
        P("row", "col"),
        P("col", "row"),
        P("row"),
        P("row"),
        P(None, "row", "col"),
        P("col", None, None),
        P("row", "col"),
    )
    out_specs = P("row", "col")

    return jax.shard_map(
        on_device, mesh=mesh, in_specs=in_specs, out_specs=out_specs, check_vma=False
    )
```

```python
import jax
import jax.numpy as jnp
from jax import lax
from jax.sharding import PartitionSpec as P


TILE = 128
HALF = 4
DEPTH = 4


def dot(a, b, precision=lax.Precision.HIGHEST):
    return jnp.dot(a, b, precision=precision, preferred_element_type=jnp.float32)


def z_groups(rows):
    return [list(range(y, rows, DEPTH)) for y in range(DEPTH)]


def y_shift(rows, by):
    return [(r // DEPTH * DEPTH + (r + by) % DEPTH, r) for r in range(rows)]


def send_y(array, rows):
    return [array] + [lax.ppermute(array, "row", y_shift(rows, by)) for by in range(1, DEPTH)]


def join_y(parts):
    y = lax.axis_index("row") % DEPTH
    whole = jnp.zeros((DEPTH,) + parts[0].shape, parts[0].dtype)
    for by, part in enumerate(parts):
        whole = lax.dynamic_update_index_in_dim(whole, part, (y + by) % DEPTH, 0)
    return whole


def scatter_z(parts, rows):
    return lax.all_to_all(parts, "row", 0, 0, axis_index_groups=z_groups(rows)).sum(axis=0)


def scatter_rows(partial_sum, rows):
    parts = partial_sum.reshape(rows, -1, partial_sum.shape[1])
    return lax.all_to_all(parts, "row", 0, 0).sum(axis=0)


def on_device(anc_factor, anc_solution, slot_row, tile_count, lower_factor, diag_inverse, rhs):
    column = lax.axis_index("col")
    rows = lax.axis_size("row")
    panels, rows_local, width = lower_factor.shape
    diag = diag_inverse[0]

    scaled = dot(lower_factor.reshape(panels * rows_local, width), diag)
    scaled = scaled.reshape(panels, rows_local, width)
    block = lambda k: lax.dynamic_index_in_dim(scaled, k, 0, keepdims=False)

    own = block(jnp.minimum(column + 1, panels - 1))
    one = block(jnp.where(column < HALF, 2, 7))
    two = block(jnp.where(column < HALF, 3, 6))
    one = lax.ppermute(one, "col", [(5, 7), (4, 3), (0, 6)])
    two = lax.ppermute(two, "col", [(4, 2), (1, 3), (0, 7)])
    upper = jnp.where(column == 2, two, one)
    upper = jnp.where((column >= 4) & (column <= 6), own, upper)
    lower = jnp.where(column == 6, one, two)
    lower = jnp.where(column <= 2, own, lower)

    def near_full(share):
        return lax.all_gather(
            share.reshape(-1, width),
            "row",
            axis=0,
            tiled=True,
            axis_index_groups=z_groups(rows),
        )

    upper = send_y(upper, rows)
    twice = jnp.concatenate([scaled[HALF:], scaled[HALF:-1]], axis=0)
    far = lax.dynamic_slice_in_dim(twice, column % HALF, HALF, 0)
    rest = send_y(jnp.concatenate([lower[None], far], axis=0), rows)
    upper_near = near_full(join_y(upper))

    alive = jnp.arange(slot_row.shape[0]) < tile_count[0] * TILE
    mine = jnp.where(alive[None, :], jnp.take(anc_solution, slot_row, axis=1), 0.0)
    chosen = lax.all_gather(mine, "col", axis=0, tiled=True)
    total = scatter_rows(dot(chosen, anc_factor), rows)
    value = dot(rhs - total, diag)
    value, rest = lax.optimization_barrier((value, rest))
    lower_near = near_full(join_y([part[0] for part in rest]))

    def solve_half(value, low, near):
        a, b, c, d = low, low + 1, low + 2, low + 3
        first, second = (low + 7) % panels, (low + 6) % panels

        def send(array, pairs):
            return lax.ppermute(array, "col", pairs)

        def times(array):
            return dot(array, near, lax.Precision.HIGH)

        got = send(value, [(d, c)]) + send(value, [(d, first)])
        term = times(jnp.where(column == d, value, got))
        value = value - jnp.where(column == c, term, 0.0)
        aside = send(term, [(d, b), (first, a)])
        got = send(value, [(c, b)]) + send(value, [(c, second)])
        term = times(got)
        last = send(term, [(second, a)])
        term, aside = lax.optimization_barrier((term, aside))
        value = value - jnp.where(column == b, term, 0.0) - aside
        term = times(send(value, [(b, a)]))
        term, last = lax.optimization_barrier((term, last))
        return value - term - last

    value = solve_half(value, HALF, upper_near)
    value, far = lax.optimization_barrier((value, [part[1:] for part in rest]))
    far_full = join_y(far).transpose(1, 0, 2, 3).reshape(-1, width)

    known = []
    for shift in range(HALF):
        pairs = [(HALF + (i + shift) % HALF, i) for i in range(HALF)]
        known.append(lax.ppermute(value, "col", pairs))
    depth = rows // DEPTH
    shares = value.shape[0]
    known = jnp.stack(known).reshape(HALF, shares, depth, -1).transpose(2, 1, 0, 3)
    known = lax.all_to_all(known, "row", 0, 0, axis_index_groups=z_groups(rows))
    term = dot(known.reshape(depth * shares, -1), far_full)
    value = value - scatter_z(term.reshape(depth, shares, width), rows)

    return solve_half(value, 0, lower_near)


def solution(mesh):
    in_specs = (
        P("row", "col"),
        P("col", "row"),
        P("row"),
        P("row"),
        P(None, "row", "col"),
        P("col", None, None),
        P("row", "col"),
    )
    out_specs = P("row", "col")

    return jax.shard_map(
        on_device, mesh=mesh, in_specs=in_specs, out_specs=out_specs, check_vma=False
    )
```

```python
import jax
import jax.numpy as jnp
from jax import lax
from jax.sharding import PartitionSpec as P


TILE = 128
HALF = 4
DEPTH = 4


def dot(a, b, precision=lax.Precision.HIGHEST):
    return jnp.dot(a, b, precision=precision, preferred_element_type=jnp.float32)


def z_groups(rows):
    return [list(range(y, rows, DEPTH)) for y in range(DEPTH)]


def y_shift(rows, by):
    return [(r // DEPTH * DEPTH + (r + by) % DEPTH, r) for r in range(rows)]


def send_y(array, rows):
    return [array] + [lax.ppermute(array, "row", y_shift(rows, by)) for by in range(1, DEPTH)]


def order_y(parts):
    y = lax.axis_index("row") % DEPTH
    rows = []
    for place in range(DEPTH):
        row = parts[place]
        for at in range(1, DEPTH):
            row = jnp.where(y == at, parts[(place - at) % DEPTH], row)
        rows.append(row)
    return jnp.stack(rows)


def join_y(parts):
    y = lax.axis_index("row") % DEPTH
    whole = jnp.zeros((DEPTH,) + parts[0].shape, parts[0].dtype)
    for by, part in enumerate(parts):
        whole = lax.dynamic_update_index_in_dim(whole, part, (y + by) % DEPTH, 0)
    return whole


def scatter_z(parts, rows):
    return lax.all_to_all(parts, "row", 0, 0, axis_index_groups=z_groups(rows)).sum(axis=0)


def scatter_y(partial_sum, rows):
    y = lax.axis_index("row") % DEPTH
    parts = partial_sum.reshape(rows // DEPTH, DEPTH, -1, partial_sum.shape[1])
    total = lax.dynamic_index_in_dim(parts, y, 1, keepdims=False)
    for by in range(1, DEPTH):
        give = lax.dynamic_index_in_dim(parts, (y + DEPTH - by) % DEPTH, 1, keepdims=False)
        total = total + lax.ppermute(give, "row", y_shift(rows, by))
    return total


def on_device(anc_factor, anc_solution, slot_row, tile_count, lower_factor, diag_inverse, rhs):
    column = lax.axis_index("col")
    rows = lax.axis_size("row")
    panels, rows_local, width = lower_factor.shape
    diag = diag_inverse[0]

    scaled = dot(lower_factor.reshape(panels * rows_local, width), diag)
    scaled = scaled.reshape(panels, rows_local, width)
    block = lambda k: lax.dynamic_index_in_dim(scaled, k, 0, keepdims=False)

    own = block(jnp.minimum(column + 1, panels - 1))
    one = block(jnp.where(column < HALF, 2, 7))
    two = block(jnp.where(column < HALF, 3, 6))
    one = lax.ppermute(one, "col", [(5, 7), (4, 3), (0, 6)])
    two = lax.ppermute(two, "col", [(4, 2), (1, 3), (0, 7)])
    upper = jnp.where(column == 2, two, one)
    upper = jnp.where((column >= 4) & (column <= 6), own, upper)
    lower = jnp.where(column == 6, one, two)
    lower = jnp.where(column <= 2, own, lower)

    def near_full(share):
        return lax.all_gather(
            share.reshape(-1, width),
            "row",
            axis=0,
            tiled=True,
            axis_index_groups=z_groups(rows),
        )

    upper = send_y(upper, rows)
    lower = send_y(lower, rows)
    upper_near = near_full(order_y(upper))

    alive = jnp.arange(slot_row.shape[0]) < tile_count[0] * TILE
    slot = jnp.where(alive, slot_row, -1)
    chooser = jnp.arange(anc_solution.shape[1])[:, None] == slot[None, :]
    mine = dot(anc_solution, chooser.astype(jnp.float32))
    chosen = lax.all_gather(mine, "col", axis=0, tiled=True)
    term = dot(chosen, anc_factor)
    term, lower = lax.optimization_barrier((term, lower))
    lower = order_y(lower)
    lower_near = near_full(lower)
    total = scatter_y(term, rows)
    twice = jnp.concatenate([scaled[HALF:], scaled[HALF:-1]], axis=0)
    far = lax.dynamic_slice_in_dim(twice, column % HALF, HALF, 0)
    total, far = lax.optimization_barrier((total, far))
    far = send_y(far, rows)
    total = scatter_z(total, rows)
    value = dot(rhs - total, diag)

    def solve_half(value, low, near):
        a, b, c, d = low, low + 1, low + 2, low + 3
        first, second = (low + 7) % panels, (low + 6) % panels

        def send(array, pairs):
            return lax.ppermute(array, "col", pairs)

        def times(array):
            return dot(array, near, lax.Precision.HIGH)

        got = send(value, [(d, c)]) + send(value, [(d, first)])
        term = times(jnp.where(column == d, value, got))
        value = value - jnp.where(column == c, term, 0.0)
        aside = send(term, [(d, b), (first, a)])
        got = send(value, [(c, b)]) + send(value, [(c, second)])
        term = times(got)
        last = send(term, [(second, a)])
        term, aside = lax.optimization_barrier((term, aside))
        value = value - jnp.where(column == b, term, 0.0) - aside
        term = times(send(value, [(b, a)]))
        term, last = lax.optimization_barrier((term, last))
        return value - term - last

    value = solve_half(value, HALF, upper_near)
    value, far = lax.optimization_barrier((value, far))
    far_full = join_y(far).transpose(1, 0, 2, 3).reshape(-1, width)

    known = []
    for shift in range(HALF):
        pairs = [(HALF + (i + shift) % HALF, i) for i in range(HALF)]
        known.append(lax.ppermute(value, "col", pairs))
    depth = rows // DEPTH
    shares = value.shape[0]
    known = jnp.stack(known).reshape(HALF, shares, depth, -1).transpose(2, 1, 0, 3)
    known = lax.all_to_all(known, "row", 0, 0, axis_index_groups=z_groups(rows))
    term = dot(known.reshape(depth * shares, -1), far_full, lax.Precision.HIGH)
    value = value - scatter_z(term.reshape(depth, shares, width), rows)

    return solve_half(value, 0, lower_near)


def solution(mesh):
    in_specs = (
        P("row", "col"),
        P("col", "row"),
        P("row"),
        P("row"),
        P(None, "row", "col"),
        P("col", None, None),
        P("row", "col"),
    )
    out_specs = P("row", "col")

    return jax.shard_map(
        on_device, mesh=mesh, in_specs=in_specs, out_specs=out_specs, check_vma=False
    )
```

```python
import jax
import jax.numpy as jnp
from jax import lax
from jax.sharding import PartitionSpec as P


TILE = 128
HALF = 4
DEPTH = 4


def dot(a, b, precision=lax.Precision.HIGHEST):
    return jnp.dot(a, b, precision=precision, preferred_element_type=jnp.float32)


def z_groups(rows):
    return [list(range(y, rows, DEPTH)) for y in range(DEPTH)]


def y_shift(rows, by):
    return [(r // DEPTH * DEPTH + (r + by) % DEPTH, r) for r in range(rows)]


def send_y(array, rows):
    return [array] + [lax.ppermute(array, "row", y_shift(rows, by)) for by in range(1, DEPTH)]


def order_y(parts):
    y = lax.axis_index("row") % DEPTH
    rows = []
    for place in range(DEPTH):
        row = parts[place]
        for at in range(1, DEPTH):
            row = jnp.where(y == at, parts[(place - at) % DEPTH], row)
        rows.append(row)
    return jnp.stack(rows)


def join_y(parts):
    y = lax.axis_index("row") % DEPTH
    whole = jnp.zeros((DEPTH,) + parts[0].shape, parts[0].dtype)
    for by, part in enumerate(parts):
        whole = lax.dynamic_update_index_in_dim(whole, part, (y + by) % DEPTH, 0)
    return whole


def scatter_z(parts, rows):
    return lax.all_to_all(parts, "row", 0, 0, axis_index_groups=z_groups(rows)).sum(axis=0)


def scatter_y(partial_sum, rows):
    y = lax.axis_index("row") % DEPTH
    parts = partial_sum.reshape(rows // DEPTH, DEPTH, -1, partial_sum.shape[1])
    total = lax.dynamic_index_in_dim(parts, y, 1, keepdims=False)
    for by in range(1, DEPTH):
        give = lax.dynamic_index_in_dim(parts, (y + DEPTH - by) % DEPTH, 1, keepdims=False)
        total = total + lax.ppermute(give, "row", y_shift(rows, by))
    return total


def on_device(anc_factor, anc_solution, slot_row, tile_count, lower_factor, diag_inverse, rhs):
    column = lax.axis_index("col")
    rows = lax.axis_size("row")
    panels, rows_local, width = lower_factor.shape
    diag = diag_inverse[0]

    scaled = dot(lower_factor.reshape(panels * rows_local, width), diag)
    scaled = scaled.reshape(panels, rows_local, width)
    block = lambda k: lax.dynamic_index_in_dim(scaled, k, 0, keepdims=False)

    own = block(jnp.minimum(column + 1, panels - 1))
    one = block(jnp.where(column < HALF, 2, 7))
    two = block(jnp.where(column < HALF, 3, 6))
    one = lax.ppermute(one, "col", [(5, 7), (4, 3), (0, 6)])
    two = lax.ppermute(two, "col", [(4, 2), (1, 3), (0, 7)])
    upper = jnp.where(column == 2, two, one)
    upper = jnp.where((column >= 4) & (column <= 6), own, upper)
    lower = jnp.where(column == 6, one, two)
    lower = jnp.where(column <= 2, own, lower)

    def near_full(share):
        return lax.all_gather(
            share.reshape(-1, width),
            "row",
            axis=0,
            tiled=True,
            axis_index_groups=z_groups(rows),
        )

    upper = send_y(upper, rows)
    lower = send_y(lower, rows)
    upper_near = near_full(order_y(upper))

    alive = jnp.arange(slot_row.shape[0]) < tile_count[0] * TILE
    slot = jnp.where(alive, slot_row, -1)
    chooser = jnp.arange(anc_solution.shape[1])[:, None] == slot[None, :]
    mine = dot(anc_solution, chooser.astype(jnp.float32))
    chosen = lax.all_gather(mine, "col", axis=0, tiled=True)
    term = dot(chosen, anc_factor)
    term, lower = lax.optimization_barrier((term, lower))
    lower = order_y(lower)
    lower_near = near_full(lower)
    total = scatter_y(term, rows)
    twice = jnp.concatenate([scaled[HALF:], scaled[HALF:-1]], axis=0)
    far = lax.dynamic_slice_in_dim(twice, column % HALF, HALF, 0)
    far, lower = lax.optimization_barrier((far, lower))
    far = send_y(far, rows)
    total = scatter_z(total, rows)
    value = dot(rhs - total, diag, lax.Precision.HIGH)

    def solve_half(value, low, near):
        a, b, c, d = low, low + 1, low + 2, low + 3
        first, second = (low + 7) % panels, (low + 6) % panels

        def send(array, pairs):
            return lax.ppermute(array, "col", pairs)

        def times(array):
            return dot(array, near, lax.Precision.HIGH)

        got = send(value, [(d, c)]) + send(value, [(d, first)])
        term = times(jnp.where(column == d, value, got))
        value = value - jnp.where(column == c, term, 0.0)
        aside = send(term, [(d, b)])
        early = send(term, [(first, a)])
        got = send(value, [(c, b)]) + send(value, [(c, second)])
        term = times(got)
        last = send(term, [(second, a)])
        term, aside = lax.optimization_barrier((term, aside))
        value = value - jnp.where(column == b, term, 0.0) - aside
        term = times(send(value, [(b, a)]))
        term, last, early = lax.optimization_barrier((term, last, early))
        return value - term - (last + early)

    value = solve_half(value, HALF, upper_near)
    value, far = lax.optimization_barrier((value, far))
    far_full = join_y(far).transpose(1, 0, 2, 3).reshape(-1, width)

    known = []
    for shift in range(HALF):
        pairs = [(HALF + (i + shift) % HALF, i) for i in range(HALF)]
        known.append(lax.ppermute(value, "col", pairs))
    depth = rows // DEPTH
    shares = value.shape[0]
    known = jnp.stack(known).reshape(HALF, shares, depth, -1).transpose(2, 1, 0, 3)
    known = lax.all_to_all(known, "row", 0, 0, axis_index_groups=z_groups(rows))
    term = dot(known.reshape(depth * shares, -1), far_full, lax.Precision.HIGH)
    value = value - scatter_z(term.reshape(depth, shares, width), rows)

    return solve_half(value, 0, lower_near)


def solution(mesh):
    in_specs = (
        P("row", "col"),
        P("col", "row"),
        P("row"),
        P("row"),
        P(None, "row", "col"),
        P("col", None, None),
        P("row", "col"),
    )
    out_specs = P("row", "col")

    return jax.shard_map(
        on_device, mesh=mesh, in_specs=in_specs, out_specs=out_specs, check_vma=False
    )
```
